32 devices in a mesh: dp: 2 (over x), seq: 8 (over z, y), head: 2 (over core).
Axes of the slice: x: 2, y: 2, z: 4, core: 2. Of those that a mesh axis runs over, the one named last changes fastest.
Arguments:
- queries: bfloat16 [3072, 2048], P(('dp', 'seq'), 'head'), parts along dimension 0, may hold values from -6 to 6
- keys: bfloat16 [3072, 2048], P(('dp', 'seq'), 'head'), parts along dimension 0, may hold values from -6 to 6
- values: bfloat16 [3072, 2048], P(('dp', 'seq'), 'head'), parts along dimension 0, may hold values from -6 to 6
- segments: int32 [3072], P(('dp', 'seq')), parts along dimension 0, may hold values from 0 to 2, never falling along the last dimension, each value on 1 to 768 neighbouring positions
- hidden_in: bfloat16 [3072, 2048], P(('dp', 'seq', 'head')), parts along dimension 0, may hold values from -6 to 6
- attn_gain: float32 [2048], P('head'), may hold values from 0.25 to 1.75
- out_proj: bfloat16 [2048, 2048], P('head', 'seq'), may hold values from -0.125 to 0.125
- moe_gain: float32 [2048], replicated, may hold values from 0.1 to 1.9
- route_ids: int32 [3072, 8], P(('dp', 'seq', 'head')), parts along dimension 0, may hold values from 0 to 15, all different within a row; in each aligned block of 96 rows (0 to 95, 96 to 191, ...) at most 64 rows name the same one
- route_w: float32 [3072, 8], P(('dp', 'seq', 'head')), parts along dimension 0, may hold values from 0.02 to 0.5
- w_gate: bfloat16 [16, 2048, 768], P(('seq', 'head')), may hold values from -0.125 to 0.125
- w_up: bfloat16 [16, 2048, 768], P(('seq', 'head')), may hold values from -0.125 to 0.125
- w_down: bfloat16 [16, 768, 2048], P(('seq', 'head')), may hold values from -0.625 to 0.625
Outputs:
- block_out: bfloat16 [3072, 2048], P(('dp', 'seq', 'head')), parts along dimension 0
The draws below stay inside these ranges and needn't reach their ends.
There are 2 independent parts, one for each index of `dp`. The reference program is written for one: setup_inputs(seed, part) draws one part's arguments, and reference() takes and returns one part's arrays. A program takes and returns all parts, laid end to end along the dimension named above; an argument that names none is the same for every part. Nothing has to cross between parts.
Inputs may be any that keep to these rules, and one draw needn't show every extreme that they name: `route_ids`: each row names 8 different experts. In the 96 rows of one device no expert is named more than 64 times; in some device's rows some expert is named exactly 64 times. `segments`: ids of 3 packed documents, never falling, every document at least one token, the longest exactly 768 tokens.
All inputs are finite; a program needn't handle non-finite values.
Results may differ from the reference program's by a relative error of at most 0.0065.
Values may be sent and summed in bfloat16 or wider, within the bound.
No kernel may reach another device: no remote copies, remote signals or barrier semaphores. Data moves between devices by JAX's collectives and lax.ppermute only.
A program may use at most 128 MiB of HBM per device.

```python
import math
import jax
import jax.numpy as jnp
import numpy as np
from jax import lax

D = 2048
DK = 128
FF = 768
TOPK = 8
HEADS = 16
DOCS = 3
TOKENS = 1536
TOK_DEV = 96
EXPERTS = 16
CAP = 64


def level_of(rng, extent, shards, least, largest):
    gain, own = 1.0, jax.random.fold_in(rng, 6)
    for dim, shards_of in shards:
        heights = jnp.exp(jax.random.uniform(jax.random.fold_in(own, dim), (shards_of,), jnp.float32, least / len(shards), largest / len(shards)))
        gain = gain * jnp.repeat(heights, extent[dim] // shards_of).reshape([-1 if axis == dim else 1 for axis in range(len(extent))])
    return gain


def length_profile(count, total, most, lean):
    loads = [(1 << 20) // math.isqrt(rank ** lean) + 1 for rank in range(2, count + 1)]
    spare, given = total - most - (count - 1), [1] * (count - 1)
    while spare > 0:
        free = [i for i in range(count - 1) if given[i] < most]
        pool, left = sum([loads[i] for i in free]), spare
        for i in free:
            extra = min(most - given[i], max(1, left * loads[i] // pool), spare)
            given[i] = given[i] + extra
            spare = spare - extra
    return np.array([most] + given)


def uneven_parts(key, number_of, total, reach, skew):
    if number_of == 2:
        one = jax.random.randint(key, (), max(1, total - reach), min(reach, total - 1) + 1)
        return jnp.stack([one, total - one])
    lengths = jnp.asarray(length_profile(number_of, total, reach, skew), jnp.int32)
    pairs = (number_of - 1) // 2
    donor, sink = lengths[1:1 + 2 * pairs:2], lengths[2:2 + 2 * pairs:2]
    slack = jnp.minimum(donor - 1, reach - sink)
    shifted = jax.random.randint(jax.random.fold_in(key, 1), (pairs,), 0, 1 << 20) % (slack + 1)
    lengths = lengths.at[1:1 + 2 * pairs:2].set(donor - shifted).at[2:2 + 2 * pairs:2].set(sink + shifted)
    return lengths[jax.random.permutation(jax.random.fold_in(key, 2), number_of)]


def shared_out(key, own, number, rows, amount, top, most, skew):
    sequence = jax.random.permutation(key, amount)
    packed, ordinary = load_shares(amount, rows * top, most, skew, True), load_shares(amount, rows * top, most, skew, False)
    places = jnp.arange(amount)

    def named(sizes, turn):
        used = int((sizes > 0).sum())
        fixed = max(1, used // 4)
        moved = fixed + (places - fixed + turn * (used - fixed)) % max(1, amount - fixed)
        return jnp.zeros((amount,), jnp.int32).at[sequence[jnp.where(places < fixed, places, moved)]].set(jnp.asarray(sizes, jnp.int32))

    sizes = jnp.where(number % 4 == 0, named(packed, number // 4), named(ordinary, number - number // 4 - 1))
    mixed = jax.random.permutation(jax.random.fold_in(own, 3), amount)
    donor, taker = mixed[0:amount // 2 * 2:2], mixed[1:amount // 2 * 2:2]
    margin = jnp.minimum(sizes[donor] - 1, most - sizes[taker]) // 2
    margin = jnp.where((donor == sequence[0]) | (taker == sequence[0]) | (sizes[taker] == 0), 0, jnp.maximum(margin, 0))
    moved = jax.random.randint(jax.random.fold_in(own, 4), (amount // 2,), 0, 1 << 20) % (margin + 1)
    sizes = sizes.at[donor].add(-moved).at[taker].add(moved)
    members = jnp.searchsorted(jnp.cumsum(sizes), jnp.arange(rows * top), side="right").astype(jnp.int32)
    table = members.reshape(top, rows).T
    table = table[jax.random.permutation(jax.random.fold_in(own, 1), rows)]
    turn = jax.random.randint(jax.random.fold_in(own, 2), (rows, 1), 0, top)
    return jnp.take_along_axis(table, (jnp.arange(top)[None, :] + turn) % top, axis=1)


def load_shares(count, total, bound, skew, full):
    weights = [(1 << 20) // math.isqrt(rank ** skew) + 1 for rank in range(1, count + 1)]
    largest = bound if full else min(bound, max(-(-total // count), total * weights[0] // sum(weights)))
    least = 1 if total - largest >= count - 1 else 0
    given, rest = [largest] + [least] * (count - 1), total - largest - least * (count - 1)
    while rest > 0:
        candidates = [i for i in range(1, count) if given[i] < largest] or [i for i in range(1, count) if given[i] < bound]
        mass, budget = sum([weights[i] for i in candidates]), rest
        for i in candidates:
            extra = min(bound - given[i], max(1, budget * weights[i] // mass), rest)
            given[i] = given[i] + extra
            rest = rest - extra
    return np.array(given)


def normal_values(key, extent, spread, most, shards=(), held_as=jnp.bfloat16):
    array = jax.random.normal(key, extent, jnp.float32) * spread
    if len(shards) > 0:
        array = level_of(key, extent, shards, -0.22, 0.18) * array
    return jnp.clip(array, min=-most, max=most).astype(held_as)


def setup_inputs(seed: int = 0, part: int = 0) -> dict:
    key_of = jax.random.split(jax.random.key(seed), 14)
    own_keys = jax.random.split(jax.random.fold_in(key_of[13], part), 14)
    queries = normal_values(own_keys[0], (TOKENS, HEADS * DK), 1.0, 6.0, ((0, 8), (1, 2)))
    keys = normal_values(own_keys[1], (TOKENS, HEADS * DK), 1.0, 6.0, ((0, 8), (1, 2)))
    values = normal_values(own_keys[2], (TOKENS, HEADS * DK), 1.0, 6.0, ((0, 8), (1, 2)))
    segments = jnp.searchsorted(jnp.cumsum(uneven_parts(own_keys[3], DOCS, TOKENS, TOKENS // 2, 0)), jnp.arange(TOKENS), side="right").astype(jnp.int32)
    hidden_in = normal_values(own_keys[4], (TOKENS, D), 1.0, 6.0, ((0, 16),))
    attn_gain = jnp.clip(1.0 + 0.15 * jax.random.normal(key_of[5], (HEADS * DK,), jnp.float32), 0.25, 1.75)
    out_proj = normal_values(key_of[6], (HEADS * DK, D), (HEADS * DK) ** -0.5, 0.125, ((0, 2), (1, 8)))
    moe_gain = jnp.clip(1.0 + 0.18 * jax.random.normal(key_of[7], (D,), jnp.float32), 0.1, 1.9)
    route_ids_keys = jax.random.split(jax.random.fold_in(own_keys[8], 1), TOKENS // TOK_DEV)
    route_ids_turns = jax.random.permutation(jax.random.fold_in(own_keys[8], 3), TOKENS // TOK_DEV)
    route_ids = jax.vmap(lambda own, number: shared_out(jax.random.fold_in(own_keys[8], 2), own, number, TOK_DEV, EXPERTS, TOPK, CAP, 3))(route_ids_keys, route_ids_turns).reshape((TOKENS, TOPK))
    route_w = jnp.clip(jnp.exp(math.log(0.5) - 3.218876 * jax.random.uniform(own_keys[9], (TOKENS, TOPK), jnp.float32) ** level_of(own_keys[9], (TOKENS, TOPK), ((0, 16),), -0.2, 0.2)), 0.02, 0.5)
    w_gate = normal_values(key_of[10], (EXPERTS, D, FF), D ** -0.5, 0.125, ((0, 16),))
    w_up = normal_values(key_of[11], (EXPERTS, D, FF), D ** -0.5, 0.125, ((0, 16),))
    w_down = normal_values(key_of[12], (EXPERTS, FF, D), (FF // 8) ** -0.5, 0.625, ((0, 16),))
    return {"queries": queries, "keys": keys, "values": values, "segments": segments, "hidden_in": hidden_in, "attn_gain": attn_gain, "out_proj": out_proj, "moe_gain": moe_gain, "route_ids": route_ids, "route_w": route_w, "w_gate": w_gate, "w_up": w_up, "w_down": w_down}


epsilon = 1e-06

def attention(queries, keys, values, segments):
    block_len = math.gcd(TOKENS, 512)
    block_count = TOKENS // block_len
    query_f = queries.astype(jnp.float32).reshape(block_count, block_len, HEADS, DK)
    key_f = keys.astype(jnp.float32).reshape(block_count, block_len, HEADS, DK)
    value_f = values.astype(jnp.float32).reshape(block_count, block_len, HEADS, DK)
    seg_blocks = segments.reshape(block_count, block_len)
    position = jnp.arange(block_len)
    causal = position[:, None] >= position[None, :]

    def block_step(carried, inputs):
        kv_state, last_seg = carried
        query_rows, key_rows, value_rows, seg_rows = inputs
        same_doc = (seg_rows[:, None] == seg_rows[None, :]) & causal
        scores = jnp.einsum('thd,shd->hts', query_rows, key_rows, precision=lax.Precision.HIGHEST)
        scores = jnp.where(same_doc[None], scores, 0.0)
        local_part = jnp.einsum('hts,shd->thd', scores, value_rows, precision=lax.Precision.HIGHEST)
        continued = (seg_rows == last_seg)[:, None, None]
        carried_part = jnp.einsum('thd,hde->the', query_rows, kv_state, precision=lax.Precision.HIGHEST)
        attn_out = local_part + jnp.where(continued, carried_part, 0.0)
        tail_mask = (seg_rows == seg_rows[-1])[:, None, None]
        tail_keys = jnp.where(tail_mask, key_rows, 0.0)
        new_state = jnp.einsum('thd,the->hde', tail_keys, value_rows, precision=lax.Precision.HIGHEST)
        new_state = new_state + jnp.where(seg_rows[-1] == last_seg, kv_state, 0.0)
        return ((new_state, seg_rows[-1]), attn_out)
    start = (jnp.zeros((HEADS, DK, DK), jnp.float32), jnp.int32(-1))
    unused, outputs = lax.scan(block_step, start, (query_f, key_f, value_f, seg_blocks))
    return outputs.reshape(TOKENS, HEADS, DK)

def reference(queries, keys, values, segments, hidden_in, attn_gain, out_proj, moe_gain, route_ids, route_w, w_gate, w_up, w_down):
    attn_raw = attention(queries, keys, values, segments)
    mean_square = lax.optimization_barrier(jnp.mean(attn_raw * attn_raw, axis=-1, keepdims=True))
    attended = attn_raw * lax.rsqrt(mean_square + epsilon) * attn_gain.reshape(HEADS, DK)
    attended = attended.astype(jnp.bfloat16).reshape(TOKENS, HEADS * DK)
    attn_out = jnp.dot(attended, out_proj, preferred_element_type=jnp.float32)
    mid = (hidden_in.astype(jnp.float32) + attn_out).astype(jnp.bfloat16)
    mid_wide = mid.astype(jnp.float32)
    mid_square = lax.optimization_barrier(jnp.mean(mid_wide * mid_wide, axis=-1, keepdims=True))
    normed = (mid_wide * lax.rsqrt(mid_square + epsilon) * moe_gain).astype(jnp.bfloat16)
    weights = route_w / lax.optimization_barrier(jnp.sum(route_w, axis=1, keepdims=True))
    max_rows = CAP * EXPERTS

    def expert_step(running, inputs):
        expert_index, gate_matrix, up_matrix, down_matrix = inputs
        route_hits = route_ids == expert_index
        weight_row = lax.optimization_barrier(jnp.sum(jnp.where(route_hits, weights, 0.0), axis=1))
        chosen = jnp.any(route_hits, axis=1)
        picked = jnp.nonzero(chosen, size=max_rows, fill_value=0)[0].astype(jnp.int32)
        live_count = jnp.sum(chosen.astype(jnp.int32))
        live_mask = jnp.arange(max_rows, dtype=jnp.int32) < live_count
        rows_in = normed[picked]
        gate_part = jnp.dot(rows_in, gate_matrix, preferred_element_type=jnp.float32)
        up_part = jnp.dot(rows_in, up_matrix, preferred_element_type=jnp.float32)
        inner = (jax.nn.silu(gate_part) * up_part).astype(jnp.bfloat16)
        expert_out = jnp.dot(inner, down_matrix, preferred_element_type=jnp.float32).astype(jnp.bfloat16)
        row_weight = jnp.where(live_mask, weight_row[picked], 0.0)
        running = running.at[picked].add(expert_out.astype(jnp.float32) * row_weight[:, None])
        return (running, None)
    indices = jnp.arange(EXPERTS, dtype=jnp.int32)
    mixture, unused = lax.scan(expert_step, jnp.zeros((TOKENS, D), jnp.float32), (indices, w_gate, w_up, w_down))
    return (mid_wide + mixture).astype(jnp.bfloat16)
```

```python
import functools

import jax
import jax.numpy as jnp
from jax import lax
from jax.experimental import pallas as pl
from jax.experimental.pallas import tpu as pltpu
from jax.sharding import PartitionSpec as P


DK = 128
EPS = 1e-06
AUX = 16
BF = jnp.bfloat16
F32 = jnp.float32
FFN_VMEM = 24 << 20
SMALL_VMEM = 16 << 20


def dot(a, b):
    return jnp.dot(a, b, preferred_element_type=F32)


def ring_of(size):
    return list(range(0, size, 2)) + list(range(size - 1, 0, -2))


def hops(size):
    ring = ring_of(size)
    ahead = [(ring[i], ring[(i + 1) % size]) for i in range(size)]
    return ahead, [(b, a) for a, b in ahead]


def swap(x):
    return lax.ppermute(x, "head", [(0, 1), (1, 0)])


def ring_gather(x, axis):
    size = lax.axis_size("seq")
    ahead, back = hops(size)
    far = size // 2
    got = {0: x}
    up = down = x
    for k in range(1, far + 1):
        if k == far:
            mid = x.shape[axis] // 2
            up = lax.slice_in_dim(up, 0, mid, axis=axis)
            down = lax.slice_in_dim(down, mid, None, axis=axis)
        up = lax.ppermute(up, "seq", ahead)
        down = lax.ppermute(down, "seq", back)
        if k == far:
            got[far] = (up, down)
        else:
            got[-k], got[k] = up, down
    return got


def pieces(h, part):
    step = min(part, DK)
    for i in range(0, DK, step):
        yield (h * DK + i) // part, (h * DK + i) % part, i, step


def column(row, rows):
    return jnp.broadcast_to(row, (8, row.shape[1])).T[:rows, :1]


def state_kernel(seg_col, k_ref, v_ref, o_ref):
    part = o_ref.shape[1] - AUX
    rows = k_ref.shape[0]
    seg = seg_col[...]
    last = seg[rows - 1 :, :]
    tail = seg == last
    for h in range(k_ref.shape[1] // DK):
        cols = slice(h * DK, (h + 1) * DK)
        k = jnp.where(tail, k_ref[:, cols].astype(F32), 0.0).astype(BF)
        state = lax.dot_general(k, v_ref[:, cols], (((0,), (0,)), ((), ())), preferred_element_type=F32)
        for to, row, at, step in pieces(h, part):
            o_ref[to, row : row + step, :] = state[at : at + step, :].astype(BF)
    mark = jnp.broadcast_to(last.astype(F32), (AUX, DK)).astype(BF)
    for to in range(o_ref.shape[0]):
        o_ref[to, part:, :] = mark


def carry_kernel(me, c_ref, aux, o_ref, prev):
    part = o_ref.shape[1] - AUX
    size = o_ref.shape[0]
    carried = jnp.zeros((part, DK), F32)
    marks = [c_ref[s, part:, :].astype(F32)[:8] for s in range(size)]
    before = jnp.full((8, DK), -1.0, F32)
    for d in range(size):
        o_ref[d, :part, :] = carried.astype(BF)
        o_ref[d, part:, :] = aux[d]
        if d > 0:
            before = jnp.where(me[0] == d, marks[d - 1], before)
            going = marks[d - 1][:1] == marks[d][:1]
            carried = jnp.where(going, carried, 0.0)
        carried = carried + c_ref[d, :part, :].astype(F32)
    prev[...] = before


def attention_kernel(prev, seg_col, seg_row, q_ref, k_ref, v_ref, e_ref, g_ref, o_ref):
    rows = q_ref.shape[0]
    part = e_ref.shape[1] - AUX
    t = lax.broadcasted_iota(jnp.int32, (rows, rows), 0)
    s = lax.broadcasted_iota(jnp.int32, (rows, rows), 1)
    seg = seg_col[...]
    same = (seg == seg_row[...]) & (t >= s)
    continued = seg.astype(F32) == prev[:1, :]
    for h in range(q_ref.shape[1] // DK):
        cols = slice(h * DK, (h + 1) * DK)
        q, v = q_ref[:, cols], v_ref[:, cols]
        score = lax.dot_general(q, k_ref[:, cols], (((1,), (1,)), ((), ())), preferred_element_type=F32)
        score = jnp.where(same, score, 0.0)
        high = score.astype(BF)
        low = (score - high.astype(F32)).astype(BF)
        entering = jnp.concatenate([e_ref[to, row : row + step, :] for to, row, _, step in pieces(h, part)], axis=0)
        raw = dot(high, v) + dot(low, v) + jnp.where(continued, dot(q, entering), 0.0)
        square = jnp.mean(raw * raw, axis=1, keepdims=True)
        o_ref[:, cols] = (raw * lax.rsqrt(square + EPS) * g_ref[:, cols]).astype(BF)


def projection_kernel(order, att, *rest):
    w_refs, keep, give = rest[:-2], rest[-2], rest[-1]
    tok = keep.shape[0]
    core = order[len(w_refs) - 1]
    width, half = w_refs[0].shape[1], att.shape[1] // 2
    x = att[...]

    def put(i, y):
        at = pl.ds(pl.multiple_of(order[i] * width, width), width)
        a, b = y[:tok], y[tok:]
        keep[:, at] = jnp.where(core == 0, a, b)
        give[:, at] = jnp.where(core == 0, b, a)

    for i, w in enumerate(w_refs[:-2]):
        put(i, dot(x, w[...]))
    put(len(w_refs) - 2, dot(x[:, :half], w_refs[-2][...]) + dot(x[:, half:], w_refs[-1][...]))


def ffn_kernel(rows, parts, which, owner, own, other, *rest):
    n = len(parts)
    x_refs, (wg, wu, wd), o_refs = rest[:n], rest[n : n + 3], rest[n + 3 : 2 * n + 3]
    xs, inner = rest[2 * n + 3 :]
    for (unit, col), x in zip(parts, x_refs):
        xs[unit * rows : (unit + 1) * rows, col : col + x.shape[1]] = x[...]
    ff, d = wd.shape[1:]
    block = 256 if ff % 256 == 0 else ff

    def hidden(j, _):
        at = pl.ds(pl.multiple_of(j * block, block), block)
        gate, up = dot(xs[...], wg[0, :, at]), dot(xs[...], wu[0, :, at])
        inner[:, at] = (gate / (1.0 + jnp.exp(-gate)) * up).astype(BF)
        return 0

    lax.fori_loop(0, ff // block, hidden, 0)
    scale = [column((own, other)[u % 2][pl.ds(owner[which[u // 2]], 1), :], rows) for u in range(2 * len(which))]
    width = 512
    o_cols = o_refs[0].shape[1]

    for start in range(0, d, o_cols):
        mine = [(unit, o) for (unit, col), o in zip(parts, o_refs) if col == start]

        def result(j, _):
            y = dot(inner[...], wd[0, :, pl.ds(pl.multiple_of(start + j * width, width), width)]).astype(BF).astype(F32)
            for unit, o in mine:
                o[:, pl.ds(pl.multiple_of(j * width, width), width)] = (y[unit * rows : (unit + 1) * rows] * scale[unit]).astype(BF)
            return 0

        lax.fori_loop(0, o_cols // width, result, 0)


VMEM = pl.BlockSpec(memory_space=pltpu.VMEM)
SMEM = pl.BlockSpec(memory_space=pltpu.SMEM)


def expert(parts, which, owner, xs, own, other, w_gate, w_up, w_down):
    rows = xs[0].shape[0]
    d, ff = w_gate.shape[1:]
    total = 2 * len(which) * rows
    return pl.pallas_call(
        functools.partial(ffn_kernel, rows, parts, which),
        in_specs=[SMEM] + [VMEM] * (5 + len(xs)),
        out_specs=[VMEM] * len(xs),
        out_shape=[jax.ShapeDtypeStruct(x.shape, BF) for x in xs],
        scratch_shapes=[pltpu.VMEM((total, d), BF), pltpu.VMEM((total, ff), BF)],
        compiler_params=pltpu.CompilerParams(vmem_limit_bytes=FFN_VMEM),
        cost_estimate=pl.CostEstimate(flops=6 * total * d * ff, bytes_accessed=4 * total * d, transcendentals=total * ff),
    )(owner, own, other, *xs, w_gate, w_up, w_down)


def local(queries, keys, values, segments, hidden_in, attn_gain, out_proj, moe_gain, route_ids, route_w, w_gate, w_up, w_down):
    size, cores = lax.axis_size("seq"), lax.axis_size("head")
    me, core = lax.axis_index("seq"), lax.axis_index("head")
    ring = ring_of(size)
    far = size // 2
    place = jnp.asarray([ring.index(i) for i in range(size)], jnp.int32)[me]
    offsets = [0] + [r for k in range(1, far) for r in (-k, k)] + [far]
    owners = jnp.asarray(ring, jnp.int32)[(place + jnp.asarray(offsets, jnp.int32)) % size]
    rows, heads = queries.shape[0], queries.shape[1] // DK
    tok, d = hidden_in.shape
    small = pltpu.CompilerParams(vmem_limit_bytes=SMALL_VMEM)

    w_got = ring_gather(out_proj, 0)
    w_parts = [w_got[r] for r in offsets[:-1]] + list(w_got[far])

    seg_col, seg_row = segments[:, None], segments[None, :]
    part = heads * DK // size
    block = jax.ShapeDtypeStruct((size, part + AUX, DK), BF)
    sent = pl.pallas_call(state_kernel, out_shape=block, compiler_params=small)(seg_col, keys, values)
    came = lax.all_to_all(sent, "seq", split_axis=0, concat_axis=0, tiled=True)

    weights = route_w / jnp.sum(route_w, axis=1, keepdims=True)
    experts = jnp.arange(size * cores, dtype=jnp.int32)
    dense = jnp.sum(jnp.where(route_ids.T[None] == experts[:, None, None], weights.T[None], 0.0), axis=1)
    dense = jnp.pad(dense, ((0, 0), (0, DK - tok))).reshape(size, cores, DK)
    high = dense.astype(BF)
    low = (dense - high.astype(F32)).astype(BF)
    aux = jnp.concatenate([high, low, jnp.zeros((size, AUX - 2 * cores, DK), BF)], axis=1)
    carried, prev = pl.pallas_call(
        carry_kernel,
        in_specs=[SMEM, VMEM, VMEM],
        out_specs=[VMEM, VMEM],
        out_shape=[block, jax.ShapeDtypeStruct((8, DK), F32)],
        compiler_params=small,
    )(me[None], came, aux)
    entering = lax.all_to_all(carried, "seq", split_axis=0, concat_axis=0, tiled=True)
    att = pl.pallas_call(
        attention_kernel, out_shape=jax.ShapeDtypeStruct((rows, heads * DK), BF), compiler_params=small
    )(prev, seg_col, seg_row, queries, keys, values, entering, attn_gain[None, :])

    scale = entering[:, part : part + cores].astype(F32) + entering[:, part + cores : part + 2 * cores].astype(F32)
    own = lax.dynamic_index_in_dim(scale, core, 1, False)
    other = swap(lax.dynamic_index_in_dim(scale, 1 - core, 1, False))

    if out_proj.shape[1] % 128:
        full = jnp.stack([w_got[r] for r in offsets[:-1]] + [jnp.concatenate(w_got[far], axis=0)])
        full = full[jnp.argsort(owners)].transpose(1, 0, 2).reshape(heads * DK, d)
        mid_row = heads * DK // 2
        w_parts, order = [full[:mid_row], full[mid_row:]], jnp.stack([jnp.int32(0), core])
    else:
        order = jnp.concatenate([owners, core[None]])
    keep, give = pl.pallas_call(
        projection_kernel,
        in_specs=[SMEM] + [VMEM] * (1 + len(w_parts)),
        out_specs=[VMEM, VMEM],
        out_shape=[jax.ShapeDtypeStruct((tok, d), F32)] * 2,
        compiler_params=small,
    )(order, att, *w_parts)
    give = swap(give)
    mid = (hidden_in.astype(F32) + (keep + give)).astype(BF).astype(F32)
    square = jnp.mean(mid * mid, axis=-1, keepdims=True)
    normed = (mid * lax.rsqrt(square + EPS) * moe_gain).astype(BF)

    x_got = ring_gather(normed, 1)
    cut = d // 2
    out = {}
    for k in range(far + 1):
        group = [0] if k == 0 else [far] if k == far else [-k, k]
        parts, xs = [], []
        for r in group:
            for i, x in enumerate(x_got[r] if r == far else (x_got[r],)):
                y = swap(x)
                parts += [(2 * group.index(r), i * cut), (2 * group.index(r) + 1, i * cut)]
                xs += [x, y]
        which = tuple(offsets.index(r) for r in group)
        ys = expert(tuple(parts), which, owners, xs, own, other, w_gate, w_up, w_down)
        i = 0
        for r in group:
            both = []
            for _ in range(2 if r == far else 1):
                both.append((ys[i], swap(ys[i + 1])))
                i += 2
            out[r] = both if r == far else both[0]

    ahead, back = hops(size)
    add = lambda *a: sum(x.astype(F32) for x in a)
    up = lax.ppermute(add(*out[far][0]).astype(BF), "seq", ahead)
    down = lax.ppermute(add(*out[far][1]).astype(BF), "seq", back)
    for k in range(far - 1, 0, -1):
        u, v = add(*out[k]), add(*out[-k])
        if k == far - 1:
            u = jnp.concatenate([u[:, :cut] + up.astype(F32), u[:, cut:]], axis=1)
            v = jnp.concatenate([v[:, :cut], v[:, cut:] + down.astype(F32)], axis=1)
        else:
            u, v = u + up.astype(F32), v + down.astype(F32)
        up = lax.ppermute(u.astype(BF), "seq", ahead)
        down = lax.ppermute(v.astype(BF), "seq", back)
    return (mid + (add(*out[0]) + add(up, down))).astype(BF)


def solution(mesh):
    rows = P(("dp", "seq", "head"), None)
    packed = P(("dp", "seq"), "head")
    expert_spec = P(("seq", "head"), None, None)
    return jax.shard_map(
        local,
        mesh=mesh,
        in_specs=(
            packed, packed, packed, P(("dp", "seq")), rows, P("head"), P("head", "seq"), P(), rows, rows,
            expert_spec, expert_spec, expert_spec,
        ),
        out_specs=rows,
        check_vma=False,
    )
```
